32 devices in a mesh: outer: 8 (over z, y), narrow: 4 (over x, core).
Axes of the slice: x: 2, y: 2, z: 4, core: 2. Of those that a mesh axis runs over, the one named last changes fastest.
Arguments:
- queries: bfloat16 [8192, 4096], P(('outer', 'narrow')), may hold values from -6 to 6
- keys: bfloat16 [8192, 4096], P(('outer', 'narrow')), may hold values from -6 to 6
- values: bfloat16 [8192, 4096], P(('outer', 'narrow')), may hold values from -6 to 6
- log_decay: float32 [32, 8192], P(None, ('outer', 'narrow')), may hold values from -0.8 to 0
- gain: float32 [4096], replicated, may hold values from 0.5 to 1.5
Outputs:
- mixed: bfloat16 [8192, 4096], P(('outer', 'narrow'))
The draws below stay inside these ranges and needn't reach their ends.
All inputs are finite; a program needn't handle non-finite values.
Results may differ from the reference program's by a relative error of at most 0.0052.
Values may be sent and summed in bfloat16 or wider, within the bound.
A program may use at most 64 MiB of HBM per device.

```python
import jax
import jax.numpy as jnp
from jax import lax

HEAD_COUNT = 32
DH = 128
TOK_DEV = 256
D = 4096
SPAN_LENGTH = 8192


def draw_log_decay(key, part):
    segments = jax.random.split(jax.random.fold_in(key, 17), 7)
    share = 0.5
    fast = jax.random.uniform(segments[0], (HEAD_COUNT,), jnp.float32) < share
    horizon = jnp.exp(jax.random.uniform(segments[1], (HEAD_COUNT,), jnp.float32, jnp.log(30.0), jnp.log(50.0)))
    slow_total = jax.random.uniform(segments[2], (HEAD_COUNT,), jnp.float32, 0.1, 0.3)
    base = jnp.where(fast, -1.0 / horizon, -slow_total / SPAN_LENGTH)
    count = SPAN_LENGTH // TOK_DEV
    block_factor = jnp.exp(jax.random.uniform(segments[3], (HEAD_COUNT, count), jnp.float32, jnp.log(0.5), jnp.log(2.0)))
    block_factor = jnp.repeat(block_factor, TOK_DEV, axis=1)
    place_factor = jax.random.uniform(segments[4], (HEAD_COUNT, SPAN_LENGTH), jnp.float32, 0.5, 1.5)
    forget_speeds = base[:, None] * block_factor * place_factor
    spike_indices = jax.random.randint(segments[5], (HEAD_COUNT, 2), 0, SPAN_LENGTH)
    forget_falls = jax.random.uniform(segments[6], (HEAD_COUNT, 2), jnp.float32, jnp.log(0.5), jnp.log(0.8))
    spike_finder = jnp.arange(SPAN_LENGTH)[None, None, :] == spike_indices[:, :, None]
    forget_spikes = jnp.sum(jnp.where(spike_finder, forget_falls[:, :, None], 0.0), axis=1)
    return (forget_speeds + forget_spikes).astype(jnp.float32)


def block_levels(key, extent, shards, least, largest):
    factor_of, own = 1.0, jax.random.fold_in(key, 6)
    for axis_at, shards_of in shards:
        steps = jnp.exp(jax.random.uniform(jax.random.fold_in(own, axis_at), (shards_of,), jnp.float32, least / len(shards), largest / len(shards)))
        factor_of = factor_of * jnp.repeat(steps, extent[axis_at] // shards_of).reshape([-1 if axis == axis_at else 1 for axis in range(len(extent))])
    return factor_of


def scatter_about(key, dims, scale, reach, pieces=(), kind=jnp.bfloat16):
    array = scale * jax.random.normal(key, dims, jnp.float32)
    if pieces:
        array = array * block_levels(key, dims, pieces, -0.22, 0.18)
    return jnp.clip(array, -reach, reach).astype(kind)


def setup_inputs(seed: int = 0) -> dict:
    key_list = jax.random.split(jax.random.key(seed), 6)
    queries = scatter_about(key_list[0], (SPAN_LENGTH, D), 1.0, 6.0, ((0, 32),))
    keys = scatter_about(key_list[1], (SPAN_LENGTH, D), 1.0, 6.0, ((0, 32),))
    values = scatter_about(key_list[2], (SPAN_LENGTH, D), 1.0, 6.0, ((0, 32),))
    log_decay = draw_log_decay(jax.random.fold_in(key_list[5], 71), 0)
    gain = jnp.clip(1.0 + 0.1 * jax.random.normal(key_list[4], (D,), jnp.float32), 0.5, 1.5)
    return {"queries": queries, "keys": keys, "values": values, "log_decay": log_decay, "gain": gain}


def reference(queries, keys, values, log_decay, gain):
    blocks = queries.shape[0] // TOK_DEV
    qall = queries.reshape(blocks, TOK_DEV, HEAD_COUNT, DH)
    kall = keys.reshape(blocks, TOK_DEV, HEAD_COUNT, DH)
    vall = values.reshape(blocks, TOK_DEV, HEAD_COUNT, DH)
    decay_all = jnp.transpose(log_decay.reshape(HEAD_COUNT, blocks, TOK_DEV), (1, 0, 2))
    gains = gain.reshape(HEAD_COUNT, DH)
    causal = jnp.arange(TOK_DEV)[:, None] >= jnp.arange(TOK_DEV)[None, :]

    def step(state, inputs):
        qblk, kblk, vblk, forget_speeds = inputs
        cum = jnp.cumsum(forget_speeds, axis=1)
        total = cum[:, -1]
        factor = jnp.exp(total[:, None] - cum).T
        decayed = (kblk.astype(jnp.float32) * factor[:, :, None]).astype(jnp.bfloat16)
        block_state = jnp.einsum('thd,the->hde', decayed.astype(jnp.float32), vblk.astype(jnp.float32))
        half = state.astype(jnp.bfloat16)
        scores = jnp.einsum('thd,shd->hts', qblk.astype(jnp.float32), kblk.astype(jnp.float32))
        spread = jnp.minimum(cum[:, :, None] - cum[:, None, :], 0.0)
        weights = jnp.where(causal[None], scores * jnp.exp(spread), 0.0).astype(jnp.bfloat16)
        inner = jnp.einsum('hts,she->the', weights.astype(jnp.float32), vblk.astype(jnp.float32))
        readout = jnp.einsum('thd,hde->the', qblk.astype(jnp.float32), half.astype(jnp.float32))
        numer = inner + readout * jnp.exp(cum).T[:, :, None]
        scale = lax.rsqrt(lax.optimization_barrier(jnp.mean(numer * numer, axis=-1, keepdims=True)) + 1e-06)
        result = (numer * scale * gains[None]).astype(jnp.bfloat16)
        fresh = jnp.exp(total)[:, None, None] * state + block_state
        return (fresh, result.reshape(TOK_DEV, HEAD_COUNT * DH))
    start = jnp.zeros((HEAD_COUNT, DH, DH), jnp.float32)
    final, outputs = lax.scan(step, start, (qall, kall, vall, decay_all))
    return outputs.reshape(blocks * TOK_DEV, HEAD_COUNT * DH)
```

```python
import functools

import jax
import jax.numpy as jnp
from jax import lax
from jax.experimental import pallas as pl
from jax.experimental.pallas import tpu as pltpu
from jax.sharding import PartitionSpec as P

MESH = pl.DeviceIdType.MESH
FAR = -1e30


def split_outer(outer):
    rows = 1
    for d in range(1, outer + 1):
        if d * d <= outer and outer % d == 0:
            rows = d
    return outer // rows, rows


def kernel(
    sizes, q_ref, k_ref, v_ref, ld_ref, gain_ref, out_ref,
    cum, decay_cols, tail_cols, head_cols, bias, inner,
    made, got1, t1, wsend, got2, t2, got3, t3, gsend, got4, csend, carried,
    send_sem, recv_sem, tsend_sem, trecv_sem,
):
    narrow, depth, rows, heads, width, unit = sizes
    tokens = q_ref.shape[0]
    own = heads // narrow
    sub = own // rows
    o, n = lax.axis_index("outer"), lax.axis_index("narrow")
    z, y = o // rows, lax.rem(o, rows)

    order = [narrow // 2 + i for i in range(narrow)]
    near = [lax.rem(n + i % narrow, narrow) for i in order if i % narrow]
    level = [lax.rem(y + i, rows) for i in range(1, rows)]
    deep = [lax.rem(z + i, depth) for i in range(1, depth)]

    barrier = pltpu.get_barrier_semaphore()
    peers = [(o, j) for j in near]
    peers += [(z * rows + j, n) for j in level]
    peers += [(j * rows + y, n) for j in deep]
    for peer in peers:
        pl.semaphore_signal(barrier, inc=1, device_id=peer, device_id_type=MESH)

    def copy(src, dst, ssem, rsem, peer):
        return pltpu.make_async_remote_copy(
            src_ref=src, dst_ref=dst, send_sem=ssem, recv_sem=rsem,
            device_id=peer, device_id_type=MESH,
        )

    total = ld_ref[...]
    lane = lax.broadcasted_iota(jnp.int32, total.shape, 1)
    step = 1
    while step < tokens:
        total = total + jnp.where(lane >= step, pltpu.roll(total, step, axis=1), 0.0)
        step *= 2
    cum[...] = total
    t1[n] = jnp.broadcast_to(total[:, tokens - 1 :], (heads, width))
    cols = jnp.concatenate([total, jnp.zeros((128 - heads, tokens), jnp.float32)], axis=0).T
    tail = jnp.exp(cols[tokens - 1 :] - cols)
    grown = jnp.exp(cols)
    for g in range(heads // unit):
        shift = (128 - g * unit) % 128
        for ref, value in ((decay_cols, cols), (tail_cols, tail), (head_cols, grown)):
            ref[g] = pltpu.roll(value, shift, axis=1) if shift else value
    at_t = lax.broadcasted_iota(jnp.int32, (tokens, tokens), 0)
    at_s = lax.broadcasted_iota(jnp.int32, (tokens, tokens), 1)
    bias[...] = jnp.where(at_t >= at_s, 0.0, FAR)

    def lanes(h):
        return pl.ds(pl.multiple_of(h * width, width), width)

    def states(j):
        def body(i, _):
            g = j * (own // unit) + i
            tails = tail_cols[g]
            for u in range(unit):
                at = lanes(g * unit + u)
                kept = k_ref[:, at].astype(jnp.float32) * tails[:, u : u + 1]
                made[j, i * unit + u] = lax.dot_general(
                    kept.astype(jnp.bfloat16), v_ref[:, at], (((0,), (0,)), ((), ())),
                    preferred_element_type=jnp.float32,
                ).astype(jnp.bfloat16)
            return 0

        lax.fori_loop(0, own // unit, body, 0)

    def within(first, last):
        def body(g, _):
            columns = decay_cols[g]
            for u in range(unit):
                h = g * unit + u
                at = lanes(h)
                scores = lax.dot_general(
                    q_ref[:, at], k_ref[:, at], (((1,), (1,)), ((), ())),
                    preferred_element_type=jnp.float32,
                )
                spread = columns[:, u : u + 1] - cum[pl.ds(h, 1), :] + bias[...]
                weights = (scores * jnp.exp(spread)).astype(jnp.bfloat16)
                inner[:, at] = jnp.dot(weights, v_ref[:, at], preferred_element_type=jnp.float32)
            return 0

        lax.fori_loop(first, last, body, 0)

    def finish(j):
        def body(i, _):
            g = j * (own // unit) + i
            grow = head_cols[g]
            for u in range(unit):
                at = lanes(g * unit + u)
                read = jnp.dot(
                    q_ref[:, at], carried[j, i * unit + u], preferred_element_type=jnp.float32
                )
                numer = inner[:, at] + read * grow[:, u : u + 1]
                mean = jnp.mean(numer * numer, axis=-1, keepdims=True)
                out_ref[:, at] = (numer * lax.rsqrt(mean + 1e-06) * gain_ref[:, at]).astype(
                    jnp.bfloat16
                )
            return 0

        lax.fori_loop(0, own // unit, body, 0)

    groups = heads // unit
    marks = [groups * c // 32 for c in (0, 12, 16, 28, 32)]

    pl.semaphore_wait(barrier, len(peers))
    pending = []

    def begin(one):
        one.start()
        pending.append(one)

    for i, j in enumerate(near):
        begin(copy(t1.at[n], t1.at[n], tsend_sem.at[0, i], trecv_sem.at[0, n], (o, j)))
    for i, j in enumerate(near):
        states(j)
        begin(copy(made.at[j], got1.at[n], send_sem.at[0, i], recv_sem.at[0, n], (o, j)))
    states(n)
    got1[n] = made[n]
    for i, j in enumerate(near):
        copy(t1.at[j], t1.at[j], tsend_sem.at[0, i], trecv_sem.at[0, j], (o, j)).wait_recv()
    group_total = t1[0]
    for j in range(1, narrow):
        group_total = group_total + t1[j]
    t2[y] = group_total
    for i, j in enumerate(level):
        begin(copy(t2.at[y], t2.at[y], tsend_sem.at[1, i], trecv_sem.at[1, y], (z * rows + j, n)))
    within(marks[0], marks[1])
    for i, j in enumerate(near):
        copy(made.at[j], got1.at[j], send_sem.at[0, i], recv_sem.at[0, j], (o, j)).wait_recv()

    def decay(ref, j, k):
        return jnp.exp(ref[j, pl.ds(n * own + k, 1), :])

    def sum_group(k, _):
        acc = got1[0, k].astype(jnp.float32)
        for j in range(1, narrow):
            acc = decay(t1, j, k) * acc + got1[j, k].astype(jnp.float32)
        wsend[k] = acc.astype(jnp.bfloat16)
        return 0

    lax.fori_loop(0, own, sum_group, 0)
    for i, j in enumerate(level):
        begin(
            copy(
                wsend.at[pl.ds(j * sub, sub)], got2.at[y], send_sem.at[1, i], recv_sem.at[1, y],
                (z * rows + j, n),
            )
        )
    got2[y] = wsend[pl.ds(y * sub, sub)]
    for i, j in enumerate(level):
        copy(t2.at[j], t2.at[j], tsend_sem.at[1, i], trecv_sem.at[1, j], (z * rows + j, n)).wait_recv()
    row_total = t2[0]
    for j in range(1, rows):
        row_total = row_total + t2[j]
    t3[z] = row_total
    for i, j in enumerate(deep):
        begin(copy(t3.at[z], t3.at[z], tsend_sem.at[2, i], trecv_sem.at[2, z], (j * rows + y, n)))
    within(marks[1], marks[2])
    for i, j in enumerate(level):
        copy(
            wsend.at[pl.ds(j * sub, sub)], got2.at[j], send_sem.at[1, i], recv_sem.at[1, j],
            (z * rows + j, n),
        ).wait_recv()

    def sum_row(k, _):
        acc = got2[0, k].astype(jnp.float32)
        for j in range(1, rows):
            acc = decay(t2, j, y * sub + k) * acc + got2[j, k].astype(jnp.float32)
        got3[z, k] = acc.astype(jnp.bfloat16)
        return 0

    lax.fori_loop(0, sub, sum_row, 0)
    for i, j in enumerate(deep):
        begin(copy(got3.at[z], got3.at[z], send_sem.at[2, i], recv_sem.at[2, z], (j * rows + y, n)))
    within(marks[2], marks[3])
    for i, j in enumerate(deep):
        copy(t3.at[j], t3.at[j], tsend_sem.at[2, i], trecv_sem.at[2, j], (j * rows + y, n)).wait_recv()
        copy(got3.at[j], got3.at[j], send_sem.at[2, i], recv_sem.at[2, j], (j * rows + y, n)).wait_recv()

    def enter_row(k, _):
        at = y * sub + k
        acc = jnp.zeros((width, width), jnp.float32)
        for j in range(depth - 1):
            new = decay(t3, j, at) * acc + got3[j, k].astype(jnp.float32)
            acc = jnp.where(j < z, new, acc)
        for j in range(rows):
            gsend[j, k] = acc.astype(jnp.bfloat16)
            acc = decay(t2, j, at) * acc + got2[j, k].astype(jnp.float32)
        return 0

    lax.fori_loop(0, sub, enter_row, 0)
    for i, j in enumerate(level):
        begin(copy(gsend.at[j], got4.at[y], send_sem.at[3, i], recv_sem.at[3, y], (z * rows + j, n)))
    got4[y] = gsend[y]
    within(marks[3], marks[4])
    for i, j in enumerate(level):
        copy(gsend.at[j], got4.at[j], send_sem.at[3, i], recv_sem.at[3, j], (z * rows + j, n)).wait_recv()

    def enter_group(k, _):
        acc = got4[k // sub, lax.rem(k, sub)].astype(jnp.float32)
        for j in range(narrow):
            csend[j, k] = acc.astype(jnp.bfloat16)
            acc = decay(t1, j, k) * acc + got1[j, k].astype(jnp.float32)
        return 0

    lax.fori_loop(0, own, enter_group, 0)
    for i, j in enumerate(near):
        begin(copy(csend.at[j], carried.at[n], send_sem.at[4, i], recv_sem.at[4, n], (o, j)))
    carried[n] = csend[n]
    finish(n)
    for i, j in enumerate(near[::-1]):
        copy(csend.at[j], carried.at[j], send_sem.at[4, i], recv_sem.at[4, j], (o, j)).wait_recv()
        finish(j)
    for one in pending:
        one.wait_send()


def on_device(mesh_sizes, queries, keys, values, log_decay, gain):
    outer, narrow = mesh_sizes
    tokens, model = queries.shape
    heads = log_decay.shape[0]
    width = model // heads
    depth, rows = split_outer(outer)
    own = heads // narrow
    sub = own // rows
    unit = min(4, own)
    half = lambda *shape: pltpu.VMEM(shape + (width, width), jnp.bfloat16)
    full = lambda *shape: pltpu.VMEM(shape, jnp.float32)
    most = max(narrow, depth, rows)
    dma = lambda *shape: pltpu.SemaphoreType.DMA(shape)
    vmem = pl.BlockSpec(memory_space=pltpu.VMEM)
    return pl.pallas_call(
        functools.partial(kernel, (narrow, depth, rows, heads, width, unit)),
        out_shape=jax.ShapeDtypeStruct(queries.shape, jnp.bfloat16),
        in_specs=[vmem] * 5,
        out_specs=vmem,
        scratch_shapes=[
            full(heads, tokens),
            full(heads // unit, tokens, 128),
            full(heads // unit, tokens, 128),
            full(heads // unit, tokens, 128),
            full(tokens, tokens),
            full(tokens, model),
            half(narrow, own),
            half(narrow, own),
            full(narrow, heads, width),
            half(own),
            half(rows, sub),
            full(rows, heads, width),
            half(depth, sub),
            full(depth, heads, width),
            half(rows, sub),
            half(rows, sub),
            half(narrow, own),
            half(narrow, own),
            dma(5, most),
            dma(5, most),
            dma(3, most),
            dma(3, most),
        ],
        compiler_params=pltpu.CompilerParams(
            collective_id=0, has_side_effects=True, vmem_limit_bytes=48 * 1024 * 1024
        ),
    )(queries, keys, values, log_decay, gain.reshape(1, model))


def solution(mesh):
    axes = ("outer", "narrow")
    block = P(axes, None)
    return jax.shard_map(
        functools.partial(on_device, tuple(mesh.shape[a] for a in axes)),
        mesh=mesh,
        in_specs=(block, block, block, P(None, axes), P()),
        out_specs=block,
        check_vma=False,
    )
```

```python
import functools

import jax
import jax.numpy as jnp
from jax import lax
from jax.experimental import pallas as pl
from jax.experimental.pallas import tpu as pltpu
from jax.sharding import PartitionSpec as P

MESH = pl.DeviceIdType.MESH
FAR = -1e30


def split_outer(outer):
    rows = 1
    for d in range(1, outer + 1):
        if d * d <= outer and outer % d == 0:
            rows = d
    return outer // rows, rows


def kernel(
    sizes, q_hbm, k_hbm, v_hbm, ld_ref, gain_ref, out_ref,
    q_ref, k_ref, v_ref, cum, decay_cols, tail_cols, head_cols, bias, inner,
    made, got1, t1, wsend, got2, t2, got3, t3, gsend, got4, csend, carried,
    load_sem, send_sem, recv_sem, tsend_sem, trecv_sem,
):
    narrow, depth, rows, heads, width, unit = sizes
    tokens = q_ref.shape[0]
    own = heads // narrow
    chunks = own // rows
    o, n = lax.axis_index("outer"), lax.axis_index("narrow")
    z, y = o // rows, lax.rem(o, rows)

    near = [lax.rem(n + i % narrow, narrow) for i in range(narrow // 2, narrow // 2 + narrow) if i % narrow]
    level = [lax.rem(y + i, rows) for i in range(1, rows)]
    deep = [lax.rem(z + i, depth) for i in range(1, depth)]
    group_at = lambda j: (o, j)
    row_at = lambda j: (z * rows + j, n)
    depth_at = lambda j: (j * rows + y, n)

    loads = [
        pltpu.make_async_copy(src, dst, load_sem.at[i])
        for i, (src, dst) in enumerate(((k_hbm, k_ref), (v_hbm, v_ref), (q_hbm, q_ref)))
    ]
    for one in loads:
        one.start()

    barrier = pltpu.get_barrier_semaphore()
    peers = [group_at(j) for j in near] + [row_at(j) for j in level] + [depth_at(j) for j in deep]
    for peer in peers:
        pl.semaphore_signal(barrier, inc=1, device_id=peer, device_id_type=MESH)

    total = ld_ref[...]
    lane = lax.broadcasted_iota(jnp.int32, total.shape, 1)
    step = 1
    while step < tokens:
        total = total + jnp.where(lane >= step, pltpu.roll(total, step, axis=1), 0.0)
        step *= 2
    cum[...] = total
    t1[n] = jnp.broadcast_to(total[:, tokens - 1 :], (heads, width))
    cols = jnp.concatenate([total, jnp.zeros((128 - heads, tokens), jnp.float32)], axis=0).T
    tail = jnp.exp(cols[tokens - 1 :] - cols)
    grown = jnp.exp(cols)
    for g in range(heads // unit):
        shift = (128 - g * unit) % 128
        for ref, value in ((decay_cols, cols), (tail_cols, tail), (head_cols, grown)):
            ref[g] = pltpu.roll(value, shift, axis=1) if shift else value
    at_t = lax.broadcasted_iota(jnp.int32, (tokens, tokens), 0)
    at_s = lax.broadcasted_iota(jnp.int32, (tokens, tokens), 1)
    bias[...] = jnp.where(at_t >= at_s, 0.0, FAR)

    def lanes(h):
        return pl.ds(pl.multiple_of(h * width, width), width)

    def states(c):
        def body(j, _):
            for r in range(rows):
                k = c * rows + r
                at = lanes(j * own + k)
                tails = tail_cols[j * (own // unit) + k // unit]
                u = k % unit
                kept = k_ref[:, at].astype(jnp.float32) * tails[:, u : u + 1]
                made[c, j, r] = lax.dot_general(
                    kept.astype(jnp.bfloat16), v_ref[:, at], (((0,), (0,)), ((), ())),
                    preferred_element_type=jnp.float32,
                ).astype(jnp.bfloat16)
            return 0

        lax.fori_loop(0, narrow, body, 0, unroll=2)

    def within(first, last):
        def body(g, _):
            columns = decay_cols[g]
            for u in range(unit):
                h = g * unit + u
                at = lanes(h)
                scores = lax.dot_general(
                    q_ref[:, at], k_ref[:, at], (((1,), (1,)), ((), ())),
                    preferred_element_type=jnp.float32,
                )
                spread = columns[:, u : u + 1] - cum[pl.ds(h, 1), :] + bias[...]
                weights = (scores * jnp.exp(spread)).astype(jnp.bfloat16)
                inner[:, at] = jnp.dot(weights, v_ref[:, at], preferred_element_type=jnp.float32)
            return 0

        lax.fori_loop(first, last, body, 0)

    def finish(c, j):
        for r in range(rows):
            k = c * rows + r
            at = lanes(j * own + k)
            grow = head_cols[j * (own // unit) + k // unit]
            u = k % unit
            read = jnp.dot(q_ref[:, at], carried[c, j, r], preferred_element_type=jnp.float32)
            numer = inner[:, at] + read * grow[:, u : u + 1]
            mean = jnp.mean(numer * numer, axis=-1, keepdims=True)
            out_ref[:, at] = (numer * lax.rsqrt(mean + 1e-06) * gain_ref[:, at]).astype(jnp.bfloat16)

    pending = []

    def begin(kind, c, src, dst, peers_of, where, mine):
        for i, j in enumerate(peers_of):
            one = pltpu.make_async_remote_copy(
                src_ref=src(j), dst_ref=dst(mine), send_sem=send_sem.at[kind, c, i],
                recv_sem=recv_sem.at[kind, c, mine], device_id=where(j), device_id_type=MESH,
            )
            one.start()
            pending.append(one)

    def arrive(kind, c, dst, peers_of, where):
        for i, j in enumerate(peers_of):
            pltpu.make_async_remote_copy(
                src_ref=dst(j), dst_ref=dst(j), send_sem=send_sem.at[kind, c, i],
                recv_sem=recv_sem.at[kind, c, j], device_id=where(j), device_id_type=MESH,
            ).wait_recv()

    def begin_total(kind, ref, mine, peers_of, where):
        for i, j in enumerate(peers_of):
            one = pltpu.make_async_remote_copy(
                src_ref=ref.at[mine], dst_ref=ref.at[mine], send_sem=tsend_sem.at[kind, i],
                recv_sem=trecv_sem.at[kind, mine], device_id=where(j), device_id_type=MESH,
            )
            one.start()
            pending.append(one)

    def arrive_total(kind, ref, peers_of, where):
        for i, j in enumerate(peers_of):
            pltpu.make_async_remote_copy(
                src_ref=ref.at[j], dst_ref=ref.at[j], send_sem=tsend_sem.at[kind, i],
                recv_sem=trecv_sem.at[kind, j], device_id=where(j), device_id_type=MESH,
            ).wait_recv()

    def decay(ref, j, k):
        return jnp.exp(ref[j, pl.ds(n * own + k, 1), :])

    def stage0(c):
        states(c)
        begin(0, c, lambda j: made.at[c, j], lambda j: got1.at[c, j], near, group_at, n)
        got1[c, n] = made[c, n]

    def stage1(c):
        arrive(0, c, lambda j: got1.at[c, j], near, group_at)
        for r in range(rows):
            acc = got1[c, 0, r].astype(jnp.float32)
            for j in range(1, narrow):
                acc = decay(t1, j, c * rows + r) * acc + got1[c, j, r].astype(jnp.float32)
            wsend[c, r] = acc.astype(jnp.bfloat16)
        begin(1, c, lambda j: wsend.at[c, j], lambda j: got2.at[c, j], level, row_at, y)
        got2[c, y] = wsend[c, y]

    def stage2(c):
        arrive(1, c, lambda j: got2.at[c, j], level, row_at)
        acc = got2[c, 0].astype(jnp.float32)
        for j in range(1, rows):
            acc = decay(t2, j, c * rows + y) * acc + got2[c, j].astype(jnp.float32)
        got3[c, z] = acc.astype(jnp.bfloat16)
        begin(2, c, lambda j: got3.at[c, z], lambda j: got3.at[c, j], deep, depth_at, z)

    def stage3(c):
        arrive(2, c, lambda j: got3.at[c, j], deep, depth_at)
        k = c * rows + y
        acc = jnp.zeros((width, width), jnp.float32)
        for j in range(depth - 1):
            new = decay(t3, j, k) * acc + got3[c, j].astype(jnp.float32)
            acc = jnp.where(j < z, new, acc)
        for j in range(rows):
            gsend[c, j] = acc.astype(jnp.bfloat16)
            if j < rows - 1:
                acc = decay(t2, j, k) * acc + got2[c, j].astype(jnp.float32)
        begin(3, c, lambda j: gsend.at[c, j], lambda j: got4.at[c, j], level, row_at, y)
        got4[c, y] = gsend[c, y]

    def stage4(c):
        arrive(3, c, lambda j: got4.at[c, j], level, row_at)
        for r in range(rows):
            acc = got4[c, r].astype(jnp.float32)
            for j in range(narrow):
                csend[c, j, r] = acc.astype(jnp.bfloat16)
                if j < narrow - 1:
                    acc = decay(t1, j, c * rows + r) * acc + got1[c, j, r].astype(jnp.float32)
        begin(4, c, lambda j: csend.at[c, j], lambda j: carried.at[c, j], near, group_at, n)
        carried[c, n] = csend[c, n]

    def stage5(c):
        arrive(4, c, lambda j: carried.at[c, j], near, group_at)

        def body(j, _):
            finish(c, j)
            return 0

        lax.fori_loop(0, narrow, body, 0, unroll=2)

    def totals1():
        arrive_total(0, t1, near, group_at)
        group_total = t1[0]
        for j in range(1, narrow):
            group_total = group_total + t1[j]
        t2[y] = group_total
        begin_total(1, t2, y, level, row_at)

    def totals2():
        arrive_total(1, t2, level, row_at)
        row_total = t2[0]
        for j in range(1, rows):
            row_total = row_total + t2[j]
        t3[z] = row_total
        begin_total(2, t3, z, deep, depth_at)

    pl.semaphore_wait(barrier, len(peers))
    begin_total(0, t1, n, near, group_at)
    loads[0].wait()
    loads[1].wait()
    for c in range(chunks):
        stage0(c)
    totals1()
    loads[2].wait()

    groups = heads // unit
    events = [(TIMES[p] + GAP * c, p, c) for p in range(5) for c in range(chunks)]
    events += [(TIMES[1] - 0.1, 5, 0), (TIMES[2] - 0.1, 6, 0)]
    early = min(groups, EARLY)
    within(0, early)
    filled = early
    for _, p, c in sorted(events):
        if p == 4 and filled < groups:
            within(filled, groups)
            filled = groups
        if p == 5:
            totals2()
        elif p == 6:
            arrive_total(2, t3, deep, depth_at)
        else:
            (stage1, stage2, stage3, stage4, stage5)[p](c)
            if filled < groups:
                within(filled, filled + 1)
                filled += 1
    for one in pending:
        one.wait_send()


TIMES = (5.4, 7.8, 12.8, 15.2, 19.6)
GAP = 2.75
EARLY = 2


def on_device(mesh_sizes, queries, keys, values, log_decay, gain):
    outer, narrow = mesh_sizes
    tokens, model = queries.shape
    heads = log_decay.shape[0]
    width = model // heads
    depth, rows = split_outer(outer)
    own = heads // narrow
    chunks = own // rows
    unit = min(4, own)
    half = lambda *shape: pltpu.VMEM(shape + (width, width), jnp.bfloat16)
    full = lambda *shape: pltpu.VMEM(shape, jnp.float32)
    most = max(narrow, depth, rows)
    dma = lambda *shape: pltpu.SemaphoreType.DMA(shape)
    vmem = pl.BlockSpec(memory_space=pltpu.VMEM)
    hbm = pl.BlockSpec(memory_space=pltpu.HBM)
    return pl.pallas_call(
        functools.partial(kernel, (narrow, depth, rows, heads, width, unit)),
        out_shape=jax.ShapeDtypeStruct(queries.shape, jnp.bfloat16),
        in_specs=[hbm] * 3 + [vmem] * 2,
        out_specs=vmem,
        scratch_shapes=[
            pltpu.VMEM((tokens, model), queries.dtype),
            pltpu.VMEM((tokens, model), queries.dtype),
            pltpu.VMEM((tokens, model), queries.dtype),
            full(heads, tokens),
            full(heads // unit, tokens, 128),
            full(heads // unit, tokens, 128),
            full(heads // unit, tokens, 128),
            full(tokens, tokens),
            full(tokens, model),
            half(chunks, narrow, rows),
            half(chunks, narrow, rows),
            full(narrow, heads, width),
            half(chunks, rows),
            half(chunks, rows),
            full(rows, heads, width),
            half(chunks, depth),
            full(depth, heads, width),
            half(chunks, rows),
            half(chunks, rows),
            half(chunks, narrow, rows),
            half(chunks, narrow, rows),
            dma(3),
            dma(5, chunks, most),
            dma(5, chunks, most),
            dma(3, most),
            dma(3, most),
        ],
        compiler_params=pltpu.CompilerParams(
            collective_id=0, has_side_effects=True, vmem_limit_bytes=48 * 1024 * 1024
        ),
    )(queries, keys, values, log_decay, gain.reshape(1, model))


def solution(mesh):
    axes = ("outer", "narrow")
    block = P(axes, None)
    return jax.shard_map(
        functools.partial(on_device, tuple(mesh.shape[a] for a in axes)),
        mesh=mesh,
        in_specs=(block, block, block, P(None, axes), P()),
        out_specs=block,
        check_vma=False,
    )
```

```python
import functools

import jax
import jax.numpy as jnp
from jax import lax
from jax.experimental import pallas as pl
from jax.experimental.pallas import tpu as pltpu
from jax.sharding import PartitionSpec as P

MESH = pl.DeviceIdType.MESH
FAR = -1e30


def split_outer(outer):
    rows = 1
    for d in range(1, outer + 1):
        if d * d <= outer and outer % d == 0:
            rows = d
    return outer // rows, rows


def kernel(
    sizes, q_hbm, k_hbm, v_hbm, ld_ref, gain_ref, out_ref,
    q_ref, k_ref, v_ref, cum, decay_cols, tail_cols, head_cols, bias, inner,
    made, pair, chip, got1, t1, wsend, got2, t2, made3, sums3, got3, t3, gsend, got4, csend, got5,
    other, carried,
    enter3, load_sem, send_sem, recv_sem, tsend_sem, trecv_sem, zsend_sem, zrecv_sem,
):
    narrow, depth, rows, heads, width, unit = sizes
    tokens = q_ref.shape[0]
    own = heads // narrow
    chunks = own // rows
    o, n = lax.axis_index("outer"), lax.axis_index("narrow")
    z, y = o // rows, lax.rem(o, rows)
    chips = narrow // 2
    x, core = n // 2, lax.rem(n, 2)
    levels = depth.bit_length() - 1

    near = [lax.rem(n + i % narrow, narrow) for i in range(narrow // 2, narrow // 2 + narrow) if i % narrow]
    partner = [1 - core]
    across = [lax.rem(x + i, chips) for i in range(1, chips)]
    level = [lax.rem(y + i, rows) for i in range(1, rows)]
    deep = [lax.rem(z + i, depth) for i in range(1, depth)]
    group_at = lambda j: (o, j)
    core_at = lambda j: (o, x * 2 + j)
    chip_at = lambda j: (o, j * 2 + core)
    row_at = lambda j: (z * rows + j, n)
    depth_at = lambda j: (j * rows + y, n)

    loads = [
        pltpu.make_async_copy(src, dst, load_sem.at[i])
        for i, (src, dst) in enumerate(((k_hbm, k_ref), (v_hbm, v_ref), (q_hbm, q_ref)))
    ]
    for one in loads:
        one.start()

    barrier = pltpu.get_barrier_semaphore()
    peers = [group_at(j) for j in near] + [row_at(j) for j in level] + [depth_at(j) for j in deep]
    for peer in peers:
        pl.semaphore_signal(barrier, inc=1, device_id=peer, device_id_type=MESH)

    total = ld_ref[...]
    lane = lax.broadcasted_iota(jnp.int32, total.shape, 1)
    step = 1
    while step < tokens:
        total = total + jnp.where(lane >= step, pltpu.roll(total, step, axis=1), 0.0)
        step *= 2
    cum[...] = total
    t1[n] = jnp.broadcast_to(total[:, tokens - 1 :], (heads, width))
    cols = jnp.concatenate([total, jnp.zeros((128 - heads, tokens), jnp.float32)], axis=0).T
    tail = jnp.exp(cols[tokens - 1 :] - cols)
    grown = jnp.exp(cols)
    for g in range(heads // unit):
        shift = (128 - g * unit) % 128
        for ref, value in ((decay_cols, cols), (tail_cols, tail), (head_cols, grown)):
            ref[g] = pltpu.roll(value, shift, axis=1) if shift else value
    at_t = lax.broadcasted_iota(jnp.int32, (tokens, tokens), 0)
    at_s = lax.broadcasted_iota(jnp.int32, (tokens, tokens), 1)
    bias[...] = jnp.where(at_t >= at_s, 0.0, FAR)

    def lanes(h):
        return pl.ds(pl.multiple_of(h * width, width), width)

    def states(c, side):
        def body(i, _):
            for r in range(rows):
                k = c * rows + r
                j = i * 2 + side
                at = lanes(j * own + k)
                tails = tail_cols[j * (own // unit) + k // unit]
                u = k % unit
                kept = k_ref[:, at].astype(jnp.float32) * tails[:, u : u + 1]
                made[c, side, i, r] = lax.dot_general(
                    kept.astype(jnp.bfloat16), v_ref[:, at], (((0,), (0,)), ((), ())),
                    preferred_element_type=jnp.float32,
                )
            return 0

        lax.fori_loop(0, chips, body, 0, unroll=2)

    def within(first, last):
        def body(g, _):
            columns = decay_cols[g]
            for u in range(unit):
                h = g * unit + u
                at = lanes(h)
                scores = lax.dot_general(
                    q_ref[:, at], k_ref[:, at], (((1,), (1,)), ((), ())),
                    preferred_element_type=jnp.float32,
                )
                spread = columns[:, u : u + 1] - cum[pl.ds(h, 1), :] + bias[...]
                weights = (scores * jnp.exp(spread)).astype(jnp.bfloat16)
                inner[:, at] = jnp.dot(weights, v_ref[:, at], preferred_element_type=jnp.float32)
            return 0

        lax.fori_loop(first, last, body, 0)

    def finish(c, side, i):
        j = i * 2 + side
        for r in range(rows):
            k = c * rows + r
            at = lanes(j * own + k)
            grow = head_cols[j * (own // unit) + k // unit]
            u = k % unit
            read = jnp.dot(q_ref[:, at], carried[c, side, i, r], preferred_element_type=jnp.float32)
            numer = inner[:, at] + read * grow[:, u : u + 1]
            mean = jnp.mean(numer * numer, axis=-1, keepdims=True)
            out_ref[:, at] = (numer * lax.rsqrt(mean + 1e-06) * gain_ref[:, at]).astype(jnp.bfloat16)

    pending = []

    def begin(kind, c, src, dst, peers_of, where, mine):
        for i, j in enumerate(peers_of):
            one = pltpu.make_async_remote_copy(
                src_ref=src(j), dst_ref=dst(mine), send_sem=send_sem.at[kind, c, i],
                recv_sem=recv_sem.at[kind, c, mine], device_id=where(j), device_id_type=MESH,
            )
            one.start()
            pending.append(one)

    def arrive(kind, c, dst, peers_of, where):
        for i, j in enumerate(peers_of):
            pltpu.make_async_remote_copy(
                src_ref=dst(j), dst_ref=dst(j), send_sem=send_sem.at[kind, c, i],
                recv_sem=recv_sem.at[kind, c, j], device_id=where(j), device_id_type=MESH,
            ).wait_recv()

    def begin_total(kind, ref, mine, peers_of, where):
        for i, j in enumerate(peers_of):
            one = pltpu.make_async_remote_copy(
                src_ref=ref.at[mine], dst_ref=ref.at[mine], send_sem=tsend_sem.at[kind, i],
                recv_sem=trecv_sem.at[kind, mine], device_id=where(j), device_id_type=MESH,
            )
            one.start()
            pending.append(one)

    def arrive_total(kind, ref, peers_of, where):
        for i, j in enumerate(peers_of):
            pltpu.make_async_remote_copy(
                src_ref=ref.at[j], dst_ref=ref.at[j], send_sem=tsend_sem.at[kind, i],
                recv_sem=trecv_sem.at[kind, j], device_id=where(j), device_id_type=MESH,
            ).wait_recv()

    def decay(ref, j, k):
        return jnp.exp(ref[j, pl.ds(n * own + k, 1), :])

    def decay_chip(j, k):
        at = pl.ds(n * own + k, 1)
        return jnp.exp(t1[j * 2, at, :] + t1[j * 2 + 1, at, :])

    def stage0(c):
        states(c, 1 - core)
        begin(0, c, lambda j: made.at[c, j], lambda j: pair.at[c, j], partner, core_at, core)
        states(c, core)
        pair[c, core] = made[c, core]

    def stage1(c):
        arrive(0, c, lambda j: pair.at[c, j], partner, core_at)
        for i in range(chips):
            for r in range(rows):
                at = pl.ds((i * 2 + core) * own + c * rows + r, 1)
                acc = jnp.exp(t1[x * 2 + 1, at, :]) * pair[c, 0, i, r] + pair[c, 1, i, r]
                chip[c, i, r] = acc.astype(chip.dtype)
        begin(1, c, lambda j: chip.at[c, j], lambda j: got1.at[c, j], across, chip_at, x)
        got1[c, x] = chip[c, x]

    def stage2(c):
        arrive(1, c, lambda j: got1.at[c, j], across, chip_at)
        for r in range(rows):
            acc = got1[c, 0, r].astype(jnp.float32)
            for j in range(1, chips):
                acc = decay_chip(j, c * rows + r) * acc + got1[c, j, r].astype(jnp.float32)
            wsend[c, r] = acc.astype(wsend.dtype)
        begin(2, c, lambda j: wsend.at[c, j], lambda j: got2.at[c, j], level, row_at, y)
        got2[c, y] = wsend[c, y]

    def sender(l):
        return lax.rem(z, 2 << l) == (1 << l) - 1

    def receiver(l):
        return lax.rem(z, 2 << l) >= (1 << l)

    def depth_copy(c, l, i, to):
        return pltpu.make_async_remote_copy(
            src_ref=made3.at[c, l], dst_ref=got3.at[c, l], send_sem=zsend_sem.at[c, l, i],
            recv_sem=zrecv_sem.at[c, l], device_id=depth_at(to), device_id_type=MESH,
        )

    def depth_send(c, l):
        @pl.when(sender(l))
        def _():
            made3[c, l] = sums3[c].astype(made3.dtype)
            for i in range(1 << l):
                depth_copy(c, l, i, lax.rem(z + 1 + i, depth)).start()

    def depth_take(c, l):
        k = c * rows + y

        @pl.when(receiver(l))
        def _():
            depth_copy(c, l, 0, lax.rem(z + depth - 1, depth)).wait_recv()
            gap = jnp.zeros((1, width), jnp.float32)
            for j in range(depth):
                inside = jnp.logical_and(j >= z - lax.rem(z, 1 << l), j <= z)
                gap = gap + jnp.where(inside, t3[j, pl.ds(n * own + k, 1), :], 0.0)
            new = got3[c, l].astype(jnp.float32)
            sums3[c] = jnp.exp(gap) * new + sums3[c]
            before = gap - t3[z, pl.ds(n * own + k, 1), :]
            enter3[c] = jnp.exp(before) * new + enter3[c]

    def stage3(c):
        arrive(2, c, lambda j: got2.at[c, j], level, row_at)
        acc = got2[c, 0].astype(jnp.float32)
        for j in range(1, rows):
            acc = decay(t2, j, c * rows + y) * acc + got2[c, j].astype(jnp.float32)
        sums3[c] = acc
        enter3[c] = jnp.zeros((width, width), jnp.float32)
        depth_send(c, 0)

    def stage4(c, l):
        depth_take(c, l)
        if l < levels - 1:
            depth_send(c, l + 1)
            return
        k = c * rows + y
        acc = enter3[c]
        for j in range(rows):
            gsend[c, j] = acc.astype(gsend.dtype)
            if j < rows - 1:
                acc = decay(t2, j, k) * acc + got2[c, j].astype(jnp.float32)
        begin(3, c, lambda j: gsend.at[c, j], lambda j: got4.at[c, j], level, row_at, y)
        got4[c, y] = gsend[c, y]

    def stage5(c):
        arrive(3, c, lambda j: got4.at[c, j], level, row_at)
        for r in range(rows):
            acc = got4[c, r].astype(jnp.float32)
            for j in range(chips):
                csend[c, j, r] = acc.astype(csend.dtype)
                if j < chips - 1:
                    acc = decay_chip(j, c * rows + r) * acc + got1[c, j, r].astype(jnp.float32)
        begin(4, c, lambda j: csend.at[c, j], lambda j: got5.at[c, j], across, chip_at, x)
        got5[c, x] = csend[c, x]

    def stage6(c):
        arrive(4, c, lambda j: got5.at[c, j], across, chip_at)
        for i in range(chips):
            for r in range(rows):
                at = pl.ds((i * 2 + core) * own + c * rows + r, 1)
                first = got5[c, i, r]
                later = jnp.exp(t1[x * 2, at, :]) * first.astype(jnp.float32) + pair[c, 0, i, r]
                first = first.astype(jnp.float32)
                other[c, i, r] = jnp.where(core == 0, later, first).astype(other.dtype)
                carried[c, core, i, r] = jnp.where(core == 0, first, later).astype(carried.dtype)
        begin(5, c, lambda j: other.at[c], lambda j: carried.at[c, core], partner, core_at, core)
        finish_side(c, core)

    def finish_side(c, side):
        def body(i, _):
            finish(c, side, i)
            return 0

        lax.fori_loop(0, chips, body, 0, unroll=2)

    def stage7(c):
        arrive(5, c, lambda j: carried.at[c, j], partner, core_at)
        finish_side(c, 1 - core)

    def totals1():
        arrive_total(0, t1, near, group_at)
        group_total = t1[0]
        for j in range(1, narrow):
            group_total = group_total + t1[j]
        t2[y] = group_total
        begin_total(1, t2, y, level, row_at)

    def totals2():
        arrive_total(1, t2, level, row_at)
        row_total = t2[0]
        for j in range(1, rows):
            row_total = row_total + t2[j]
        t3[z] = row_total
        begin_total(2, t3, z, deep, depth_at)

    pl.semaphore_wait(barrier, len(peers))
    begin_total(0, t1, n, near, group_at)
    loads[0].wait()
    loads[1].wait()
    for c in range(chunks):
        stage0(c)
    totals1()
    loads[2].wait()

    groups = heads // unit
    slots = [stage1, stage2, stage3]
    slots += [functools.partial(lambda l, c: stage4(c, l), l) for l in range(levels)]
    slots += [stage5, stage6, stage7]
    gaps = STEPS[:3] + (STEPS[3],) * levels + STEPS[4:]
    times = [sum(gaps[: p + 1]) for p in range(len(slots))]
    events = [(times[p] + GAP * c, p, c) for p in range(len(slots)) for c in range(chunks)]
    early = min(groups, EARLY)
    within(0, early)
    filled = early
    for _, p, c in sorted(events):
        if slots[p] is stage6 and filled < groups:
            within(filled, groups)
            filled = groups
        if slots[p] is stage3 and c == 0:
            totals2()
        if p == 3 and c == 0:
            arrive_total(2, t3, deep, depth_at)
        slots[p](c)
        if filled < groups:
            within(filled, filled + 1)
            filled += 1
    for one in pending:
        one.wait_send()
    for l in range(levels):

        @pl.when(sender(l))
        def _():
            for c in range(chunks):
                for i in range(1 << l):
                    depth_copy(c, l, i, lax.rem(z + 1 + i, depth)).wait_send()


STEPS = (2.5, 3.0, 2.3, 2.4, 2.3, 3.0, 1.5)
GAP = 1.6
EARLY = 0


def on_device(mesh_sizes, queries, keys, values, log_decay, gain):
    outer, narrow = mesh_sizes
    tokens, model = queries.shape
    heads = log_decay.shape[0]
    width = model // heads
    depth, rows = split_outer(outer)
    own = heads // narrow
    chunks = own // rows
    unit = min(4, own)
    half = lambda *shape: pltpu.VMEM(shape + (width, width), jnp.bfloat16)
    wide = lambda *shape: pltpu.VMEM(shape + (width, width), jnp.float32)
    chips = narrow // 2
    levels = depth.bit_length() - 1
    full = lambda *shape: pltpu.VMEM(shape, jnp.float32)
    most = max(narrow, depth, rows)
    dma = lambda *shape: pltpu.SemaphoreType.DMA(shape)
    vmem = pl.BlockSpec(memory_space=pltpu.VMEM)
    hbm = pl.BlockSpec(memory_space=pltpu.HBM)
    return pl.pallas_call(
        functools.partial(kernel, (narrow, depth, rows, heads, width, unit)),
        out_shape=jax.ShapeDtypeStruct(queries.shape, jnp.bfloat16),
        in_specs=[hbm] * 3 + [vmem] * 2,
        out_specs=vmem,
        scratch_shapes=[
            pltpu.VMEM((tokens, model), queries.dtype),
            pltpu.VMEM((tokens, model), queries.dtype),
            pltpu.VMEM((tokens, model), queries.dtype),
            full(heads, tokens),
            full(heads // unit, tokens, 128),
            full(heads // unit, tokens, 128),
            full(heads // unit, tokens, 128),
            full(tokens, tokens),
            full(tokens, model),
            wide(chunks, 2, chips, rows),
            wide(chunks, 2, chips, rows),
            half(chunks, chips, rows),
            half(chunks, chips, rows),
            full(narrow, heads, width),
            half(chunks, rows),
            half(chunks, rows),
            full(rows, heads, width),
            half(chunks, levels),
            wide(chunks),
            half(chunks, levels),
            full(depth, heads, width),
            half(chunks, rows),
            half(chunks, rows),
            half(chunks, chips, rows),
            half(chunks, chips, rows),
            half(chunks, chips, rows),
            half(chunks, 2, chips, rows),
            wide(chunks),
            dma(3),
            dma(6, chunks, most),
            dma(6, chunks, most),
            dma(3, most),
            dma(3, most),
            dma(chunks, levels, depth),
            dma(chunks, levels),
        ],
        compiler_params=pltpu.CompilerParams(
            collective_id=0, has_side_effects=True, vmem_limit_bytes=60 * 1024 * 1024
        ),
    )(queries, keys, values, log_decay, gain.reshape(1, model))


def solution(mesh):
    axes = ("outer", "narrow")
    block = P(axes, None)
    return jax.shard_map(
        functools.partial(on_device, tuple(mesh.shape[a] for a in axes)),
        mesh=mesh,
        in_specs=(block, block, block, P(None, axes), P()),
        out_specs=block,
        check_vma=False,
    )
```

```python
import functools

import jax
import jax.numpy as jnp
from jax import lax
from jax.experimental import pallas as pl
from jax.experimental.pallas import tpu as pltpu
from jax.sharding import PartitionSpec as P

MESH = pl.DeviceIdType.MESH
FAR = -1e30


def split_outer(outer):
    rows = 1
    for d in range(1, outer + 1):
        if d * d <= outer and outer % d == 0:
            rows = d
    return outer // rows, rows


def kernel(
    sizes, q_hbm, k_hbm, v_hbm, ld_ref, gain_ref, out_ref,
    q_ref, k_ref, v_ref, cum, decay_cols, tail_cols, head_cols, bias, inner,
    made, got1, t1, wsend, got2, t2, got3, t3, gsend, got4, csend, carried,
    load_sem, send_sem, recv_sem, tsend_sem, trecv_sem,
):
    narrow, depth, rows, heads, width, unit = sizes
    tokens = q_ref.shape[0]
    own = heads // narrow
    chunks = own // rows
    o, n = lax.axis_index("outer"), lax.axis_index("narrow")
    z, y = o // rows, lax.rem(o, rows)

    near = [lax.rem(n + i % narrow, narrow) for i in range(narrow // 2, narrow // 2 + narrow) if i % narrow]
    level = [lax.rem(y + i, rows) for i in range(1, rows)]
    deep = [lax.rem(z + i, depth) for i in range(1, depth)]
    group_at = lambda j: (o, j)
    row_at = lambda j: (z * rows + j, n)
    depth_at = lambda j: (j * rows + y, n)

    loads = [
        pltpu.make_async_copy(src, dst, load_sem.at[i])
        for i, (src, dst) in enumerate(((k_hbm, k_ref), (v_hbm, v_ref), (q_hbm, q_ref)))
    ]
    for one in loads:
        one.start()

    barrier = pltpu.get_barrier_semaphore()
    peers = [group_at(j) for j in near] + [row_at(j) for j in level] + [depth_at(j) for j in deep]
    for peer in peers:
        pl.semaphore_signal(barrier, inc=1, device_id=peer, device_id_type=MESH)

    total = ld_ref[...]
    lane = lax.broadcasted_iota(jnp.int32, total.shape, 1)
    step = 1
    while step < tokens:
        total = total + jnp.where(lane >= step, pltpu.roll(total, step, axis=1), 0.0)
        step *= 2
    cum[...] = total
    t1[n] = jnp.broadcast_to(total[:, tokens - 1 :], (heads, width))
    cols = jnp.concatenate([total, jnp.zeros((128 - heads, tokens), jnp.float32)], axis=0).T
    tail = jnp.exp(cols[tokens - 1 :] - cols)
    grown = jnp.exp(cols)
    for g in range(heads // unit):
        shift = (128 - g * unit) % 128
        for ref, value in ((decay_cols, cols), (tail_cols, tail), (head_cols, grown)):
            ref[g] = pltpu.roll(value, shift, axis=1) if shift else value
    at_t = lax.broadcasted_iota(jnp.int32, (tokens, tokens), 0)
    at_s = lax.broadcasted_iota(jnp.int32, (tokens, tokens), 1)
    bias[...] = jnp.where(at_t >= at_s, 0.0, FAR)

    def lanes(h):
        return pl.ds(pl.multiple_of(h * width, width), width)

    def states(c):
        def body(j, _):
            for r in range(rows):
                k = c * rows + r
                at = lanes(j * own + k)
                tails = tail_cols[j * (own // unit) + k // unit]
                u = k % unit
                kept = k_ref[:, at].astype(jnp.float32) * tails[:, u : u + 1]
                made[c, j, r] = lax.dot_general(
                    kept.astype(jnp.bfloat16), v_ref[:, at], (((0,), (0,)), ((), ())),
                    preferred_element_type=jnp.float32,
                ).astype(jnp.bfloat16)
            return 0

        lax.fori_loop(0, narrow, body, 0, unroll=2)

    def within(first, last):
        def body(g, _):
            columns = decay_cols[g]
            for u in range(unit):
                h = g * unit + u
                at = lanes(h)
                scores = lax.dot_general(
                    q_ref[:, at], k_ref[:, at], (((1,), (1,)), ((), ())),
                    preferred_element_type=jnp.float32,
                )
                spread = columns[:, u : u + 1] - cum[pl.ds(h, 1), :] + bias[...]
                weights = (scores * jnp.exp(spread)).astype(jnp.bfloat16)
                inner[:, at] = jnp.dot(weights, v_ref[:, at], preferred_element_type=jnp.float32)
            return 0

        lax.fori_loop(first, last, body, 0)

    def finish(c, j):
        for r in range(rows):
            k = c * rows + r
            at = lanes(j * own + k)
            grow = head_cols[j * (own // unit) + k // unit]
            u = k % unit
            read = jnp.dot(q_ref[:, at], carried[c, j, r], preferred_element_type=jnp.float32)
            numer = inner[:, at] + read * grow[:, u : u + 1]
            mean = jnp.mean(numer * numer, axis=-1, keepdims=True)
            out_ref[:, at] = (numer * lax.rsqrt(mean + 1e-06) * gain_ref[:, at]).astype(jnp.bfloat16)

    pending = []

    def begin(kind, c, src, dst, peers_of, where, mine):
        for i, j in enumerate(peers_of):
            one = pltpu.make_async_remote_copy(
                src_ref=src(j), dst_ref=dst(mine), send_sem=send_sem.at[kind, c, i],
                recv_sem=recv_sem.at[kind, c, mine], device_id=where(j), device_id_type=MESH,
            )
            one.start()
            pending.append(one)

    def arrive(kind, c, dst, peers_of, where):
        for i, j in enumerate(peers_of):
            pltpu.make_async_remote_copy(
                src_ref=dst(j), dst_ref=dst(j), send_sem=send_sem.at[kind, c, i],
                recv_sem=recv_sem.at[kind, c, j], device_id=where(j), device_id_type=MESH,
            ).wait_recv()

    def begin_total(kind, ref, mine, peers_of, where):
        for i, j in enumerate(peers_of):
            one = pltpu.make_async_remote_copy(
                src_ref=ref.at[mine], dst_ref=ref.at[mine], send_sem=tsend_sem.at[kind, i],
                recv_sem=trecv_sem.at[kind, mine], device_id=where(j), device_id_type=MESH,
            )
            one.start()
            pending.append(one)

    def arrive_total(kind, ref, peers_of, where):
        for i, j in enumerate(peers_of):
            pltpu.make_async_remote_copy(
                src_ref=ref.at[j], dst_ref=ref.at[j], send_sem=tsend_sem.at[kind, i],
                recv_sem=trecv_sem.at[kind, j], device_id=where(j), device_id_type=MESH,
            ).wait_recv()

    def decay(ref, j, k):
        return jnp.exp(ref[j, pl.ds(n * own + k, 1), :])

    def stage0(c):
        states(c)
        begin(0, c, lambda j: made.at[c, j], lambda j: got1.at[c, j], near, group_at, n)
        got1[c, n] = made[c, n]

    def stage1(c):
        arrive(0, c, lambda j: got1.at[c, j], near, group_at)
        for r in range(rows):
            acc = got1[c, 0, r].astype(jnp.float32)
            for j in range(1, narrow):
                acc = decay(t1, j, c * rows + r) * acc + got1[c, j, r].astype(jnp.float32)
            wsend[c, r] = acc.astype(jnp.bfloat16)
        begin(1, c, lambda j: wsend.at[c, j], lambda j: got2.at[c, j], level, row_at, y)
        got2[c, y] = wsend[c, y]

    def stage2(c):
        arrive(1, c, lambda j: got2.at[c, j], level, row_at)
        acc = got2[c, 0].astype(jnp.float32)
        for j in range(1, rows):
            acc = decay(t2, j, c * rows + y) * acc + got2[c, j].astype(jnp.float32)
        got3[c, z] = acc.astype(jnp.bfloat16)
        begin(2, c, lambda j: got3.at[c, z], lambda j: got3.at[c, j], deep, depth_at, z)

    def stage3(c):
        arrive(2, c, lambda j: got3.at[c, j], deep, depth_at)
        k = c * rows + y
        acc = jnp.zeros((width, width), jnp.float32)
        for j in range(depth - 1):
            new = decay(t3, j, k) * acc + got3[c, j].astype(jnp.float32)
            acc = jnp.where(j < z, new, acc)
        for j in range(rows):
            gsend[c, j] = acc.astype(jnp.bfloat16)
            if j < rows - 1:
                acc = decay(t2, j, k) * acc + got2[c, j].astype(jnp.float32)
        begin(3, c, lambda j: gsend.at[c, j], lambda j: got4.at[c, j], level, row_at, y)
        got4[c, y] = gsend[c, y]

    def stage4(c):
        arrive(3, c, lambda j: got4.at[c, j], level, row_at)
        for r in range(rows):
            acc = got4[c, r].astype(jnp.float32)
            for j in range(narrow):
                csend[c, j, r] = acc.astype(jnp.bfloat16)
                if j < narrow - 1:
                    acc = decay(t1, j, c * rows + r) * acc + got1[c, j, r].astype(jnp.float32)
        begin(4, c, lambda j: csend.at[c, j], lambda j: carried.at[c, j], near, group_at, n)
        carried[c, n] = csend[c, n]

    def stage5(c):
        arrive(4, c, lambda j: carried.at[c, j], near, group_at)

        def body(j, _):
            finish(c, j)
            return 0

        lax.fori_loop(0, narrow, body, 0, unroll=2)

    def totals1():
        arrive_total(0, t1, near, group_at)
        group_total = t1[0]
        for j in range(1, narrow):
            group_total = group_total + t1[j]
        t2[y] = group_total
        begin_total(1, t2, y, level, row_at)

    def totals2():
        arrive_total(1, t2, level, row_at)
        row_total = t2[0]
        for j in range(1, rows):
            row_total = row_total + t2[j]
        t3[z] = row_total
        begin_total(2, t3, z, deep, depth_at)

    pl.semaphore_wait(barrier, len(peers))
    begin_total(0, t1, n, near, group_at)
    loads[0].wait()
    loads[1].wait()
    for c in range(chunks):
        stage0(c)
    totals1()
    loads[2].wait()

    groups = heads // unit
    events = [(TIMES[p] + GAP * c, p, c) for p in range(5) for c in range(chunks)]
    events += [(TIMES[1] - 0.1, 5, 0), (TIMES[2] - 0.1, 6, 0)]
    early = min(groups, EARLY)
    within(0, early)
    filled = early
    for _, p, c in sorted(events):
        if p == 4 and filled < groups:
            within(filled, groups)
            filled = groups
        if p == 5:
            totals2()
        elif p == 6:
            arrive_total(2, t3, deep, depth_at)
        else:
            (stage1, stage2, stage3, stage4, stage5)[p](c)
            if filled < groups:
                within(filled, filled + 1)
                filled += 1
    for one in pending:
        one.wait_send()


TIMES = (5.4, 7.8, 12.8, 15.2, 19.6)
GAP = 2.75
EARLY = 0


def on_device(mesh_sizes, queries, keys, values, log_decay, gain):
    outer, narrow = mesh_sizes
    tokens, model = queries.shape
    heads = log_decay.shape[0]
    width = model // heads
    depth, rows = split_outer(outer)
    own = heads // narrow
    chunks = own // rows
    unit = min(4, own)
    half = lambda *shape: pltpu.VMEM(shape + (width, width), jnp.bfloat16)
    full = lambda *shape: pltpu.VMEM(shape, jnp.float32)
    most = max(narrow, depth, rows)
    dma = lambda *shape: pltpu.SemaphoreType.DMA(shape)
    vmem = pl.BlockSpec(memory_space=pltpu.VMEM)
    hbm = pl.BlockSpec(memory_space=pltpu.HBM)
    return pl.pallas_call(
        functools.partial(kernel, (narrow, depth, rows, heads, width, unit)),
        out_shape=jax.ShapeDtypeStruct(queries.shape, jnp.bfloat16),
        in_specs=[hbm] * 3 + [vmem] * 2,
        out_specs=vmem,
        scratch_shapes=[
            pltpu.VMEM((tokens, model), queries.dtype),
            pltpu.VMEM((tokens, model), queries.dtype),
            pltpu.VMEM((tokens, model), queries.dtype),
            full(heads, tokens),
            full(heads // unit, tokens, 128),
            full(heads // unit, tokens, 128),
            full(heads // unit, tokens, 128),
            full(tokens, tokens),
            full(tokens, model),
            half(chunks, narrow, rows),
            half(chunks, narrow, rows),
            full(narrow, heads, width),
            half(chunks, rows),
            half(chunks, rows),
            full(rows, heads, width),
            half(chunks, depth),
            full(depth, heads, width),
            half(chunks, rows),
            half(chunks, rows),
            half(chunks, narrow, rows),
            half(chunks, narrow, rows),
            dma(3),
            dma(5, chunks, most),
            dma(5, chunks, most),
            dma(3, most),
            dma(3, most),
        ],
        compiler_params=pltpu.CompilerParams(
            collective_id=0, has_side_effects=True, vmem_limit_bytes=60 * 1024 * 1024
        ),
    )(queries, keys, values, log_decay, gain.reshape(1, model))


def solution(mesh):
    axes = ("outer", "narrow")
    block = P(axes, None)
    return jax.shard_map(
        functools.partial(on_device, tuple(mesh.shape[a] for a in axes)),
        mesh=mesh,
        in_specs=(block, block, block, P(None, axes), P()),
        out_specs=block,
        check_vma=False,
    )
```
